32 devices in a mesh: dp: 8 (over y, x, core), tensor: 4 (over z).
Axes of the slice: x: 2, y: 2, z: 4, core: 2. Of those that a mesh axis runs over, the one named last changes fastest.
Arguments:
- inputs: bfloat16 [6144, 2048], P('dp', 'tensor'), may hold values from -6 to 6
- labels: int32 [6144], P('dp'), may hold values from 0 to 1
- cotangent: bfloat16 [6144, 2048], P('dp', 'tensor'), may hold values from -6 to 6
- gate_weight: bfloat16 [2048, 2], P('tensor'), may hold values from -0.125 to 0.125
- weight_in: bfloat16 [3, 2048, 4096], P(None, None, 'tensor'), may hold values from -0.125 to 0.125
- weight_out: bfloat16 [3, 4096, 2048], P(None, 'tensor'), may hold values from -0.09375 to 0.09375
Outputs:
- input_grad: float32 [6144, 2048], P('dp', 'tensor')
- gate_grad: float32 [2048, 2], P('tensor')
- weight_in_grad: float32 [3, 2048, 4096], P(None, 'dp', 'tensor')
- weight_out_grad: float32 [3, 4096, 2048], P(None, 'tensor', 'dp')
The draws below stay inside these ranges and needn't reach their ends.
All inputs are finite; a program needn't handle non-finite values.
Results may differ from the reference program's by a relative error of at most 0.0075.
Values may be sent and summed in bfloat16 or wider, within the bound.
A program may use at most 192 MiB of HBM per device.

```python
import jax
import jax.numpy as jnp
from jax import lax

D = 2048
HID = 4096
TASKS = 2
EXPERTS = 3
TOKENS = 6144


def set_ends(drawn, key, smallest, high):
    longest = drawn.shape.index(max(drawn.shape))
    spots = []
    for shift in (0, 1):
        where = [jax.random.randint(jax.random.fold_in(key, axis), (), 0, length) for axis, length in enumerate(drawn.shape)]
        where[longest] = (where[longest] + shift) % drawn.shape[longest]
        spots.append(tuple(where))
    return drawn.at[spots[0]].set(smallest).at[spots[1]].set(high)


def strengthened(entries, own_key, source, target, parts, factor):
    owner, partner = [(jnp.arange(entries.shape[position]) // (entries.shape[position] // parts)).reshape([-1 if axis == position else 1 for axis in range(entries.ndim)]) for position in (source, target)]
    chosen = jax.random.permutation(own_key, parts)[partner]
    strong = (owner == chosen) | (owner == (partner + parts // 2) % parts)
    return jnp.where(strong, factor * entries, entries)


def levels(own_key, shape, shards, smallest, high):
    gain, own = 1.0, jax.random.fold_in(own_key, 6)
    for dim, blocks in shards:
        heights = jnp.exp(jax.random.uniform(jax.random.fold_in(own, dim), (blocks,), jnp.float32, smallest / len(shards), high / len(shards)))
        gain = gain * jnp.repeat(heights, shape[dim] // blocks).reshape([-1 if axis == dim else 1 for axis in range(len(shape))])
    return gain


def scatter_about(stream_key, dims, spread, reach, shards=(), kind=jnp.bfloat16):
    gain = levels(stream_key, dims, shards, -0.22, 0.18) if shards else 1.0
    values = jax.random.normal(stream_key, dims, jnp.float32) * spread * gain
    return jnp.minimum(jnp.maximum(values, -reach), reach).astype(kind)


def gaussian_with(rng, shape, spread, most, shards, heavy, kind=jnp.bfloat16):
    result = spread * jax.random.normal(rng, shape, jnp.float32)
    if shards:
        result = result * levels(rng, shape, shards, -0.22, 0.18)
    return jnp.clip(strengthened(result, jax.random.fold_in(rng, 3), *heavy), -most, most).astype(kind)


def setup_inputs(seed: int = 0) -> dict:
    keys = jax.random.split(jax.random.key(seed), 7)
    inputs = gaussian_with(keys[0], (TOKENS, D), 1.0, 6.0, ((0, 8), (1, 4)), (0, 1, 8, 2.0))
    labels = set_ends(jax.random.randint(keys[1], (TOKENS,), 0, TASKS), jax.random.fold_in(keys[1], 1), 0, TASKS - 1).astype(jnp.int32)
    cotangent = gaussian_with(keys[2], (TOKENS, D), 1.0, 6.0, ((0, 8), (1, 4)), (0, 1, 8, 2.0))
    gate_weight = scatter_about(keys[3], (D, TASKS), D ** -0.5, 0.125, ((0, 4),))
    weight_in = scatter_about(keys[4], (EXPERTS, D, HID), D ** -0.5, 0.125, ((2, 4),))
    weight_out = scatter_about(keys[5], (EXPERTS, HID, D), HID ** -0.5, 0.09375, ((1, 4),))
    return dict(inputs=inputs, labels=labels, cotangent=cotangent, gate_weight=gate_weight, weight_in=weight_in, weight_out=weight_out)


def reference(inputs, labels, cotangent, gate_weight, weight_in, weight_out):
    contract_rows = (((0,), (0,)), ((), ()))
    contract_cols = (((1,), (1,)), ((), ()))
    logits = jnp.dot(inputs, gate_weight, preferred_element_type=jnp.float32)
    picked = (labels[:, None] == jnp.arange(TASKS, dtype=jnp.int32)[None, :]).astype(jnp.float32)
    task_gate = jax.nn.sigmoid(jnp.sum(logits * picked, axis=1))
    mixing = jnp.concatenate([(1.0 - task_gate)[:, None], task_gate[:, None] * picked], axis=1)
    cot_float = cotangent.astype(jnp.float32)
    scores = []
    grads_in = []
    grads_out = []
    input_grad = None
    for expert in range(EXPERTS):
        hidden = jnp.dot(inputs, weight_in[expert], preferred_element_type=jnp.float32)
        sigma = jax.nn.sigmoid(hidden)
        active = (hidden * sigma).astype(jnp.bfloat16)
        back_grad = lax.dot_general(cotangent, weight_out[expert], contract_cols, preferred_element_type=jnp.float32)
        scores.append(jnp.sum(active.astype(jnp.float32) * back_grad, axis=1))
        share = mixing[:, expert:expert + 1]
        hidden_grad = (share * back_grad * sigma * (1.0 + hidden * (1.0 - sigma))).astype(jnp.bfloat16)
        out_grad = (share * cot_float).astype(jnp.bfloat16)
        term = lax.dot_general(hidden_grad, weight_in[expert], contract_cols, preferred_element_type=jnp.float32)
        input_grad = term if input_grad is None else input_grad + term
        grads_in.append(lax.dot_general(inputs, hidden_grad, contract_rows, preferred_element_type=jnp.float32))
        grads_out.append(lax.dot_general(active, out_grad, contract_rows, preferred_element_type=jnp.float32))
    score = jnp.stack(scores, axis=1)
    own = jnp.sum(score[:, 1:] * picked, axis=1) - score[:, 0]
    slope = task_gate * (1.0 - task_gate) * own
    slope_rows = slope[:, None] * picked
    input_grad = input_grad + jnp.dot(slope_rows, gate_weight.astype(jnp.float32).T, precision=lax.Precision.HIGHEST)
    gate_grad = jnp.dot(inputs.astype(jnp.float32).T, slope_rows, precision=lax.Precision.HIGHEST)
    return input_grad, gate_grad, jnp.stack(grads_in), jnp.stack(grads_out)
```

```python
import jax
import jax.numpy as jnp
from jax import lax
from jax.sharding import PartitionSpec as P


ROWS = (((0,), (0,)), ((), ()))
COLS = (((1,), (1,)), ((), ()))


def relative_order(order):
    offsets = [0]
    for bit in reversed(order):
        offsets = offsets + [offset + bit for offset in offsets]
    return offsets


def pieces(array, order, count):
    width = array.shape[1] // count
    me = lax.axis_index("dp")
    blocks = [
        lax.dynamic_slice_in_dim(array, (me ^ offset) * width, width, axis=1)
        for offset in relative_order(order)
    ]
    parts, size = [blocks[0]], 1
    while size < count:
        parts.append(jnp.concatenate(blocks[size : 2 * size], axis=1))
        size *= 2
    return parts


def scatter_sum(product, parts, order, count, axis):
    arrived = []

    def partial(index):
        total = product(parts[index])
        start = 0 if index == 0 else total.shape[axis]
        for block in arrived:
            total = total + lax.slice_in_dim(
                block, start, start + total.shape[axis], axis=axis
            ).astype(jnp.float32)
        return total

    for step, bit in enumerate(order):
        sent = partial(len(order) - step).astype(jnp.bfloat16)
        arrived.append(
            lax.ppermute(sent, "dp", [(device, device ^ bit) for device in range(count)])
        )
    return partial(0)


def ring_gather(block, size):
    if size == 1:
        return block
    ahead = [(place, (place + 1) % size) for place in range(size)]
    behind = [(place, (place - 1) % size) for place in range(size)]
    me = lax.axis_index("tensor")
    width = block.shape[1]
    held = {0: block}
    left, right = block, block
    for step in range(1, (size + 1) // 2):
        left = held[-step] = lax.ppermute(left, "tensor", ahead)
        right = held[step] = lax.ppermute(right, "tensor", behind)
    if size % 2 == 0:
        half = block.shape[0] // 2
        top = lax.ppermute(left[:half], "tensor", ahead)
        bottom = lax.ppermute(right[half:], "tensor", behind)
        held[size // 2] = jnp.concatenate([top, bottom], axis=0)
    full = jnp.zeros((block.shape[0], width * size), block.dtype)
    for shift, part in held.items():
        place = (me + shift + size) % size
        full = lax.dynamic_update_slice_in_dim(full, part, place * width, axis=1)
    return full


def shards(count, size, inputs, labels, cotangent, gate_weight, weight_in, weight_out):
    num_tasks = gate_weight.shape[1]
    num_experts = weight_in.shape[0]
    bits = [1 << place for place in range(count.bit_length() - 1)]
    order_in, order_out = bits, bits[:1] + bits[:0:-1]
    gate_full = lax.all_gather(gate_weight.T, "tensor", axis=1, tiled=True)
    x_full = ring_gather(inputs, size)
    cot_full = ring_gather(cotangent, size)
    logits = lax.dot_general(x_full, gate_full, COLS, preferred_element_type=jnp.float32)
    picked = (labels[:, None] == jnp.arange(num_tasks, dtype=jnp.int32)[None, :]).astype(
        jnp.float32
    )
    task_gate = jax.nn.sigmoid(jnp.sum(logits * picked, axis=1))
    mixing = jnp.concatenate([(1.0 - task_gate)[:, None], task_gate[:, None] * picked], axis=1)
    x_parts = pieces(x_full, order_in, count)
    cot_parts = pieces(cot_full, order_out, count)
    scores, grads_in, grads_out = [], [], []
    partial_input = None
    for expert in range(num_experts):
        hidden = jnp.dot(x_full, weight_in[expert], preferred_element_type=jnp.float32)
        sigma = jax.nn.sigmoid(hidden)
        active = (hidden * sigma).astype(jnp.bfloat16)
        back_grad = lax.dot_general(
            cot_full, weight_out[expert], COLS, preferred_element_type=jnp.float32
        )
        scores.append(jnp.sum(active.astype(jnp.float32) * back_grad, axis=1))
        share = mixing[:, expert : expert + 1]
        hidden_grad = (share * back_grad * sigma * (1.0 + hidden * (1.0 - sigma))).astype(
            jnp.bfloat16
        )

        def product_in(part, hidden_grad=hidden_grad):
            return lax.dot_general(part, hidden_grad, ROWS, preferred_element_type=jnp.float32)

        def product_out(part, active=active, share=share):
            out_grad = (share * part.astype(jnp.float32)).astype(jnp.bfloat16)
            return lax.dot_general(active, out_grad, ROWS, preferred_element_type=jnp.float32)

        grads_out.append(scatter_sum(product_out, cot_parts, order_out, count, 1))
        grads_in.append(scatter_sum(product_in, x_parts, order_in, count, 0))
        term = lax.dot_general(
            hidden_grad, weight_in[expert], COLS, preferred_element_type=jnp.float32
        )
        partial_input = term if partial_input is None else partial_input + term
    own_part = jnp.sum(jnp.stack(scores[1:], axis=1) * picked, axis=1) - scores[0]
    own = jnp.sum(lax.all_gather(own_part, "tensor"), axis=0)
    slope = task_gate * (1.0 - task_gate) * own
    slope_rows = slope[:, None] * picked
    input_grad = lax.psum_scatter(
        partial_input.astype(jnp.bfloat16), "tensor", scatter_dimension=1, tiled=True
    ).astype(jnp.float32)
    input_grad = input_grad + jnp.dot(
        slope_rows, gate_weight.astype(jnp.float32).T, precision=lax.Precision.HIGHEST
    )
    gate_part = jnp.dot(slope_rows.T, inputs.astype(jnp.float32), precision=lax.Precision.HIGHEST)
    gate_grad = jnp.sum(lax.all_gather(gate_part, "dp"), axis=0).T
    return (input_grad, gate_grad, jnp.stack(grads_in), jnp.stack(grads_out))


def solution(mesh):
    count, size = mesh.shape["dp"], mesh.shape["tensor"]
    in_specs = (
        P("dp", "tensor"),
        P("dp"),
        P("dp", "tensor"),
        P("tensor", None),
        P(None, None, "tensor"),
        P(None, "tensor", None),
    )
    out_specs = (
        P("dp", "tensor"),
        P("tensor", None),
        P(None, "dp", "tensor"),
        P(None, "tensor", "dp"),
    )

    def body(*args):
        return shards(count, size, *args)

    return jax.shard_map(body, mesh=mesh, in_specs=in_specs, out_specs=out_specs, check_vma=False)
```

```python
import jax
import jax.numpy as jnp
from jax import lax
from jax.sharding import PartitionSpec as P


ROWS = (((0,), (0,)), ((), ()))
COLS = (((1,), (1,)), ((), ()))


def relative_order(order):
    offsets = [0]
    for bit in reversed(order):
        offsets = offsets + [offset + bit for offset in offsets]
    return offsets


def after(value, *others):
    return lax.optimization_barrier((value, *others))[0]


def pieces(array, axis_name, order):
    count = 1 << len(order)
    width = array.shape[1] // count
    me = lax.axis_index(axis_name)
    blocks = [
        lax.dynamic_slice_in_dim(array, (me ^ offset) * width, width, axis=1)
        for offset in relative_order(order)
    ]
    parts, size = [blocks[0]], 1
    while size < count:
        parts.append(jnp.concatenate(blocks[size : 2 * size], axis=1))
        size *= 2
    return parts


def exchange(value, axis_name, bit, count):
    return lax.ppermute(value, axis_name, [(device, device ^ bit) for device in range(count)])


def butterfly_sum(value, axis_name, count):
    bit = 1
    while bit < count:
        value = value + exchange(value, axis_name, bit, count)
        bit *= 2
    return value


class Halving:
    def __init__(self, product, parts, axis_name, order, axis):
        self.product, self.parts, self.axis_name = product, parts, axis_name
        self.order, self.axis = order, axis
        self.arrived, self.sent = [], None

    def partial(self, index, *behind):
        part = after(self.parts[index], *behind) if behind else self.parts[index]
        total = self.product(part)
        length = total.shape[self.axis]
        start = 0 if index == 0 else length
        for block in self.arrived:
            total = total + lax.slice_in_dim(
                block, start, start + length, axis=self.axis
            ).astype(jnp.float32)
        return total

    def round(self, *behind):
        step = len(self.arrived)
        self.sent = self.partial(len(self.order) - step, *behind).astype(jnp.bfloat16)
        self.arrived.append(
            exchange(self.sent, self.axis_name, self.order[step], 1 << len(self.order))
        )
        return self.sent

    def result(self):
        return self.partial(0)


def ring_start(block, size):
    ahead = [(place, (place + 1) % size) for place in range(size)]
    behind = [(place, (place - 1) % size) for place in range(size)]
    return lax.ppermute(block, "tensor", ahead), lax.ppermute(block, "tensor", behind)


def ring_finish(block, left, right, size):
    ahead = [(place, (place + 1) % size) for place in range(size)]
    behind = [(place, (place - 1) % size) for place in range(size)]
    me = lax.axis_index("tensor")
    width = block.shape[1]
    held = {0: block}
    for step in range(1, (size + 1) // 2):
        if step > 1:
            left = lax.ppermute(left, "tensor", ahead)
            right = lax.ppermute(right, "tensor", behind)
        held[-step], held[step] = left, right
    half = block.shape[0] // 2
    top = lax.ppermute(left[:half], "tensor", ahead)
    bottom = lax.ppermute(right[half:], "tensor", behind)
    held[size // 2] = jnp.concatenate([top, bottom], axis=0)
    full = jnp.zeros((block.shape[0], width * size), block.dtype)
    for shift, part in held.items():
        place = (me + shift + size) % size
        full = lax.dynamic_update_slice_in_dim(full, part, place * width, axis=1)
    return full


def shards(count, size, inputs, labels, cotangent, gate_weight, weight_in, weight_out):
    num_tasks = gate_weight.shape[1]
    num_experts = weight_in.shape[0]
    bits = [1 << place for place in range(count.bit_length() - 1)]
    order_in, order_out = bits, bits[:1] + bits[:0:-1]
    order_tensor = [1 << place for place in range(size.bit_length() - 1)]

    x_left, x_right = ring_start(inputs, size)
    x_full = ring_finish(inputs, x_left, x_right, size)
    cot_own = after(cotangent, x_left, x_right)
    cot_full = ring_finish(cot_own, *ring_start(cot_own, size), size)

    picked = (labels[:, None] == jnp.arange(num_tasks, dtype=jnp.int32)[None, :]).astype(
        jnp.float32
    )
    logits = jnp.dot(inputs, gate_weight, preferred_element_type=jnp.float32)
    task_gate = jax.nn.sigmoid(butterfly_sum(jnp.sum(logits * picked, axis=1), "tensor", size))
    mixing = jnp.concatenate([(1.0 - task_gate)[:, None], task_gate[:, None] * picked], axis=1)

    hiddens = [
        jnp.dot(x_full, weight_in[expert], preferred_element_type=jnp.float32)
        for expert in range(num_experts)
    ]
    *hiddens, cot_full = lax.optimization_barrier((*hiddens, cot_full))
    x_parts = pieces(x_full, "dp", order_in)
    cot_parts = pieces(cot_full, "dp", order_out)
    scores, sums_in, sums_out, behind = [], [], [], []
    partial_input = None
    for expert in range(num_experts):
        hidden = hiddens[expert]
        sigma = jax.nn.sigmoid(hidden)
        active = (hidden * sigma).astype(jnp.bfloat16)
        share = mixing[:, expert : expert + 1]

        def product_out(part, active=active, share=share):
            out_grad = (share * part.astype(jnp.float32)).astype(jnp.bfloat16)
            return lax.dot_general(active, out_grad, ROWS, preferred_element_type=jnp.float32)

        sum_out = Halving(product_out, cot_parts, "dp", order_out, 1)
        first = sum_out.round(*behind)
        back_grad = lax.dot_general(
            after(cot_full, first), weight_out[expert], COLS, preferred_element_type=jnp.float32
        )
        scores.append(jnp.sum(active.astype(jnp.float32) * back_grad, axis=1))
        hidden_grad = (share * back_grad * sigma * (1.0 + hidden * (1.0 - sigma))).astype(
            jnp.bfloat16
        )

        def product_in(part, hidden_grad=hidden_grad):
            return lax.dot_general(part, hidden_grad, ROWS, preferred_element_type=jnp.float32)

        sum_in = Halving(product_in, x_parts, "dp", order_in, 0)
        behind = [sum_in.round()]
        if sums_in:
            behind = [sums_out[-1].round(*behind), sums_in[-1].round(*behind)]
        term = lax.dot_general(
            hidden_grad, weight_in[expert], COLS, preferred_element_type=jnp.float32
        )
        partial_input = term if partial_input is None else partial_input + term
        sums_in.append(sum_in)
        sums_out.append(sum_out)
    sums_out[-1].round()
    sums_in[-1].round()
    total_input = Halving(
        lambda part: part, pieces(partial_input, "tensor", order_tensor), "tensor", order_tensor, 1
    )
    for _ in order_tensor:
        total_input.round()
    for _ in order_in[2:]:
        for sum_out, sum_in in zip(sums_out, sums_in):
            sum_out.round()
            sum_in.round()
    grads_in = [sum_in.result() for sum_in in sums_in]
    grads_out = [sum_out.result() for sum_out in sums_out]

    own_part = jnp.sum(jnp.stack(scores[1:], axis=1) * picked, axis=1) - scores[0]
    own = butterfly_sum(own_part, "tensor", size)
    slope = task_gate * (1.0 - task_gate) * own
    slope_rows = slope[:, None] * picked
    input_grad = total_input.result() + jnp.dot(
        slope_rows, gate_weight.astype(jnp.float32).T, precision=lax.Precision.HIGHEST
    )
    gate_part = jnp.dot(slope_rows.T, inputs.astype(jnp.float32), precision=lax.Precision.HIGHEST)
    gate_grad = butterfly_sum(gate_part, "dp", count).T
    return (input_grad, gate_grad, jnp.stack(grads_in), jnp.stack(grads_out))


def solution(mesh):
    count, size = mesh.shape["dp"], mesh.shape["tensor"]
    in_specs = (
        P("dp", "tensor"),
        P("dp"),
        P("dp", "tensor"),
        P("tensor", None),
        P(None, None, "tensor"),
        P(None, "tensor", None),
    )
    out_specs = (
        P("dp", "tensor"),
        P("tensor", None),
        P(None, "dp", "tensor"),
        P(None, "tensor", "dp"),
    )

    def body(*args):
        return shards(count, size, *args)

    return jax.shard_map(body, mesh=mesh, in_specs=in_specs, out_specs=out_specs, check_vma=False)
```

```python
import jax
import jax.numpy as jnp
from jax import lax
from jax.sharding import PartitionSpec as P


ROWS = (((0,), (0,)), ((), ()))
COLS = (((1,), (1,)), ((), ()))


def relative_order(order):
    offsets = [0]
    for bit in reversed(order):
        offsets = offsets + [offset + bit for offset in offsets]
    return offsets


def after(value, *others):
    return lax.optimization_barrier((value, *others))[0]


def pieces(array, axis_name, order):
    count = 1 << len(order)
    width = array.shape[1] // count
    me = lax.axis_index(axis_name)
    blocks = [
        lax.dynamic_slice_in_dim(array, (me ^ offset) * width, width, axis=1)
        for offset in relative_order(order)
    ]
    parts, size = [blocks[0]], 1
    while size < count:
        parts.append(jnp.concatenate(blocks[size : 2 * size], axis=1))
        size *= 2
    return parts


def exchange(value, axis_name, bit, count):
    return lax.ppermute(value, axis_name, [(device, device ^ bit) for device in range(count)])


def butterfly_sum(value, axis_name, count):
    bit = 1
    while bit < count:
        value = value + exchange(value, axis_name, bit, count)
        bit *= 2
    return value


class Halving:
    def __init__(self, product, parts, axis_name, order, axis):
        self.product, self.parts, self.axis_name = product, parts, axis_name
        self.order, self.axis = order, axis
        self.arrived, self.sent = [], None

    def partial(self, index, *behind):
        part = after(self.parts[index], *behind) if behind else self.parts[index]
        total = self.product(part)
        length = total.shape[self.axis]
        start = 0 if index == 0 else length
        for block in self.arrived:
            total = total + lax.slice_in_dim(
                block, start, start + length, axis=self.axis
            ).astype(jnp.float32)
        return total

    def round(self, *behind):
        step = len(self.arrived)
        self.sent = self.partial(len(self.order) - step, *behind).astype(jnp.bfloat16)
        self.arrived.append(
            exchange(self.sent, self.axis_name, self.order[step], 1 << len(self.order))
        )
        return self.sent

    def result(self):
        return self.partial(0)


def ring_start(block, size):
    ahead = [(place, (place + 1) % size) for place in range(size)]
    behind = [(place, (place - 1) % size) for place in range(size)]
    return lax.ppermute(block, "tensor", ahead), lax.ppermute(block, "tensor", behind)


def ring_finish(block, left, right, size):
    ahead = [(place, (place + 1) % size) for place in range(size)]
    behind = [(place, (place - 1) % size) for place in range(size)]
    me = lax.axis_index("tensor")
    width = block.shape[1]
    held = {0: block}
    for step in range(1, (size + 1) // 2):
        if step > 1:
            left = lax.ppermute(left, "tensor", ahead)
            right = lax.ppermute(right, "tensor", behind)
        held[-step], held[step] = left, right
    half = block.shape[0] // 2
    top = lax.ppermute(left[:half], "tensor", ahead)
    bottom = lax.ppermute(right[half:], "tensor", behind)
    held[size // 2] = jnp.concatenate([top, bottom], axis=0)
    full = jnp.zeros((block.shape[0], width * size), block.dtype)
    for shift, part in held.items():
        place = (me + shift + size) % size
        full = lax.dynamic_update_slice_in_dim(full, part, place * width, axis=1)
    return full


def shards(count, size, inputs, labels, cotangent, gate_weight, weight_in, weight_out):
    num_tasks = gate_weight.shape[1]
    num_experts = weight_in.shape[0]
    bits = [1 << place for place in range(count.bit_length() - 1)]
    order_in, order_out = bits, bits[:1] + bits[:0:-1]
    order_tensor = [1 << place for place in range(size.bit_length() - 1)]

    x_left, x_right = ring_start(inputs, size)
    x_full = ring_finish(inputs, x_left, x_right, size)
    cot_own = after(cotangent, x_left, x_right)
    cot_left, cot_right = ring_start(cot_own, size)
    cot_full = ring_finish(cot_own, cot_left, cot_right, size)
    x_full = after(x_full, cot_left, cot_right)

    picked = (labels[:, None] == jnp.arange(num_tasks, dtype=jnp.int32)[None, :]).astype(
        jnp.float32
    )
    logits = jnp.dot(inputs, gate_weight, preferred_element_type=jnp.float32)
    task_gate = jax.nn.sigmoid(butterfly_sum(jnp.sum(logits * picked, axis=1), "tensor", size))
    mixing = jnp.concatenate([(1.0 - task_gate)[:, None], task_gate[:, None] * picked], axis=1)

    hiddens = [
        jnp.dot(x_full, weight_in[expert], preferred_element_type=jnp.float32)
        for expert in range(num_experts)
    ]
    *hiddens, cot_full = lax.optimization_barrier((*hiddens, cot_full))
    x_parts = pieces(x_full, "dp", order_in)
    cot_parts = pieces(cot_full, "dp", order_out)
    scores, sums_in, sums_out, behind = [], [], [], []
    partial_input = None
    for expert in range(num_experts):
        hidden = hiddens[expert]
        sigma = jax.nn.sigmoid(hidden)
        active = (hidden * sigma).astype(jnp.bfloat16)
        share = mixing[:, expert : expert + 1]

        def product_out(part, active=active, share=share):
            out_grad = (share * part.astype(jnp.float32)).astype(jnp.bfloat16)
            return lax.dot_general(active, out_grad, ROWS, preferred_element_type=jnp.float32)

        sum_out = Halving(product_out, cot_parts, "dp", order_out, 1)
        first = sum_out.round(*behind)
        back_grad = lax.dot_general(
            after(cot_full, first), weight_out[expert], COLS, preferred_element_type=jnp.float32
        )
        scores.append(jnp.sum(active.astype(jnp.float32) * back_grad, axis=1))
        hidden_grad = (share * back_grad * sigma * (1.0 + hidden * (1.0 - sigma))).astype(
            jnp.bfloat16
        )

        def product_in(part, hidden_grad=hidden_grad):
            return lax.dot_general(part, hidden_grad, ROWS, preferred_element_type=jnp.float32)

        sum_in = Halving(product_in, x_parts, "dp", order_in, 0)
        behind = [sum_in.round()]
        if sums_in:
            behind = [sums_out[-1].round(*behind), sums_in[-1].round(*behind)]
        term = lax.dot_general(
            hidden_grad, weight_in[expert], COLS, preferred_element_type=jnp.float32
        )
        partial_input = term if partial_input is None else partial_input + term
        sums_in.append(sum_in)
        sums_out.append(sum_out)
    sums_out[-1].round()
    sums_in[-1].round()
    total_input = Halving(
        lambda part: part, pieces(partial_input, "tensor", order_tensor), "tensor", order_tensor, 1
    )
    for _ in order_tensor:
        total_input.round()
    for _ in order_in[2:]:
        for sum_out, sum_in in zip(sums_out, sums_in):
            sum_out.round()
            sum_in.round()
    grads_in = [sum_in.result() for sum_in in sums_in]
    grads_out = [sum_out.result() for sum_out in sums_out]

    own_part = jnp.sum(jnp.stack(scores[1:], axis=1) * picked, axis=1) - scores[0]
    own = butterfly_sum(own_part, "tensor", size)
    slope = task_gate * (1.0 - task_gate) * own
    slope_rows = slope[:, None] * picked
    input_grad = total_input.result() + jnp.dot(
        slope_rows, gate_weight.astype(jnp.float32).T, precision=lax.Precision.HIGHEST
    )
    gate_part = jnp.dot(slope_rows.T, inputs.astype(jnp.float32), precision=lax.Precision.HIGHEST)
    gate_grad = butterfly_sum(gate_part, "dp", count).T
    return (input_grad, gate_grad, jnp.stack(grads_in), jnp.stack(grads_out))


def solution(mesh):
    count, size = mesh.shape["dp"], mesh.shape["tensor"]
    in_specs = (
        P("dp", "tensor"),
        P("dp"),
        P("dp", "tensor"),
        P("tensor", None),
        P(None, None, "tensor"),
        P(None, "tensor", None),
    )
    out_specs = (
        P("dp", "tensor"),
        P("tensor", None),
        P(None, "dp", "tensor"),
        P(None, "tensor", "dp"),
    )

    def body(*args):
        return shards(count, size, *args)

    return jax.shard_map(
        body, mesh=mesh, in_specs=in_specs, out_specs=out_specs, check_vma=False
    )
```
